32 devices in a mesh: fsdp: 32 (over z, y, x, core).
Axes of the slice: x: 2, y: 2, z: 4, core: 2. Of those that a mesh axis runs over, the one named last changes fastest.
Arguments:
- inputs: bfloat16 [16384, 768], P('fsdp'), may hold values from -6 to 6
- cotangent: bfloat16 [16384, 768], P('fsdp'), may hold values from -6 to 6
- norm_gain: bfloat16 [2, 768], P(None, 'fsdp'), may hold values from 0.5 to 1.5
- in_w: bfloat16 [2, 768, 3248], P(None, 'fsdp'), may hold values from -0.21875 to 0.21875
- conv_w: bfloat16 [2, 4, 1664], P(None, None, 'fsdp'), may hold values from -3 to 3
- conv_b: bfloat16 [2, 1664], P(None, 'fsdp'), may hold values from -3 to 3
- dt_bias: float32 [2, 48], replicated, may hold values from -4.5 to -1
- a_log: float32 [2, 24], replicated, may hold values from -1.5 to 1
- skip: float32 [2, 24], replicated, may hold values from 0.5 to 1.5
- fc_d: bfloat16 [2, 1536, 24], P(None, 'fsdp'), may hold values from -0.15625 to 0.15625
- inner_gain: bfloat16 [2, 1536], P(None, 'fsdp'), may hold values from 0.5 to 1.5
- out_w: bfloat16 [2, 1536, 768], P(None, 'fsdp'), may hold values from -0.15625 to 0.15625
Outputs:
- output: float32 [16384, 768], P('fsdp')
- input_grad: float32 [16384, 768], P('fsdp')
- grad_norm_gain: float32 [2, 768], P(None, 'fsdp')
- grad_in_w: float32 [2, 768, 3248], P(None, 'fsdp')
- grad_conv_w: float32 [2, 4, 1664], P(None, None, 'fsdp')
- grad_conv_b: float32 [2, 1664], P(None, 'fsdp')
- grad_dt_bias: float32 [2, 48], replicated
- grad_a_log: float32 [2, 24], replicated
- grad_skip: float32 [2, 24], replicated
- grad_fc_d: float32 [2, 1536, 24], P(None, 'fsdp')
- grad_inner_gain: float32 [2, 1536], P(None, 'fsdp')
- grad_out_w: float32 [2, 1536, 768], P(None, 'fsdp')
The draws below stay inside these ranges and needn't reach their ends.
All inputs are finite; a program needn't handle non-finite values.
Results may differ from the reference program's by a relative error of at most 0.012.
The reference program's roundings to bfloat16 on the way count: a program that leaves them out, or rounds other values in their place, can miss the bound.
Values may be sent and summed in bfloat16 or wider, within the bound.
No kernel may reach another device: no remote copies, remote signals or barrier semaphores. Data moves between devices by JAX's collectives and lax.ppermute only.
A program may use at most 384 MiB of HBM per device.

```python
import jax
import jax.numpy as jnp
from jax import lax

D = 768
INNER = 1536
CONV = 4
GROUP = 128
LAYERS = 2
SEQ = 512
HEADS = 24
CW = 1664
PROJ = 3248
TOKENS = 16384
N_FSDP = 32


def spiked(entries, own_key, source, target, parts, factor):
    def block_of(axis_at):
        return (jnp.arange(entries.shape[axis_at]) // (entries.shape[axis_at] // parts)).reshape((-1,) + (1,) * (entries.ndim - 1 - axis_at))

    near = jax.random.permutation(own_key, parts)[block_of(target)]
    far = (block_of(target) + parts // 2) % parts
    return jnp.where((block_of(source) == near) | (block_of(source) == far), factor * entries, entries)


def block_levels(rng, shape, shards, least, top_value):
    level, own = 1.0, jax.random.fold_in(rng, 6)
    for dim, parts in shards:
        draws = jnp.exp(jax.random.uniform(jax.random.fold_in(own, dim), (parts,), jnp.float32, least / len(shards), top_value / len(shards)))
        level = level * jnp.repeat(draws, shape[dim] // parts).reshape([-1 if axis == dim else 1 for axis in range(len(shape))])
    return level


def noise(key, extent, deviation, bound, cuts=(), dtype=jnp.bfloat16):
    drawn = jax.random.normal(key, extent, jnp.float32) * deviation
    if len(cuts) > 0:
        drawn = block_levels(key, extent, cuts, -0.22, 0.18) * drawn
    return jnp.clip(drawn, min=-bound, max=bound).astype(dtype)


def noise_with(key, extent, scale, limit, pieces, heavy, kind=jnp.bfloat16):
    entries = scale * jax.random.normal(key, extent, jnp.float32)
    if pieces:
        entries = entries * block_levels(key, extent, pieces, -0.22, 0.18)
    return jnp.clip(spiked(entries, jax.random.fold_in(key, 3), *heavy), -limit, limit).astype(kind)


def setup_inputs(seed: int = 0) -> dict:
    arg_keys = jax.random.split(jax.random.key(seed), 13)
    inputs = noise_with(arg_keys[0], (TOKENS, D), 1.0, 6.0, ((0, 32),), (0, 1, 32, 2.75))
    cotangent = noise(arg_keys[1], (TOKENS, D), 1.0, 6.0, ((0, 32),))
    norm_gain = jnp.clip(1.0 + 0.1 * jax.random.normal(arg_keys[2], (LAYERS, D), jnp.float32), 0.5, 1.5).astype(jnp.bfloat16)
    in_w = noise(arg_keys[3], (LAYERS, D, PROJ), D ** -0.5, 0.21875, ((1, 32),))
    conv_w = noise(arg_keys[4], (LAYERS, CONV, CW), CONV ** -0.5, 3.0, ((2, 32),))
    conv_b = noise(arg_keys[5], (LAYERS, CW), 0.5, 3.0, ((1, 32),))
    dt_bias = jnp.clip(jax.random.uniform(arg_keys[6], (LAYERS, 2 * HEADS), jnp.float32, -4.5, -1.0), -4.5, -1.0)
    a_log = jnp.clip(jax.random.uniform(arg_keys[7], (LAYERS, HEADS), jnp.float32, -1.5, 1.0), -1.5, 1.0)
    skip = jnp.clip(jax.random.uniform(arg_keys[8], (LAYERS, HEADS), jnp.float32, 0.5, 1.5), 0.5, 1.5)
    fc_d = noise(arg_keys[9], (LAYERS, INNER, HEADS), INNER ** -0.5, 0.15625, ((1, 32),))
    inner_gain = jnp.clip(1.0 + 0.1 * jax.random.normal(arg_keys[10], (LAYERS, INNER), jnp.float32), 0.5, 1.5).astype(jnp.bfloat16)
    out_w = noise(arg_keys[11], (LAYERS, INNER, D), INNER ** -0.5, 0.15625, ((1, 32),))
    return dict(inputs=inputs, cotangent=cotangent, norm_gain=norm_gain, in_w=in_w, conv_w=conv_w, conv_b=conv_b, dt_bias=dt_bias, a_log=a_log, skip=skip, fc_d=fc_d, inner_gain=inner_gain, out_w=out_w)


@jax.custom_vjp
def low(v):
    return lax.optimization_barrier(v.astype(jnp.bfloat16)).astype(jnp.float32)

@jax.custom_vjp
def low_back(v):
    return v

def low_keep(v):
    return (low(v), None)

def low_pass(kept, grad):
    return (grad,)

def back_keep(v):
    return (v, None)

def back_low(kept, grad):
    return (low(grad),)
low.defvjp(low_keep, low_pass)
low_back.defvjp(back_keep, back_low)
epsilon = 1e-05
highest = lax.Precision.HIGHEST

def rms_scale(values, gain):
    return values * lax.rsqrt(lax.optimization_barrier(jnp.mean(values * values, axis=-1, keepdims=True)) + epsilon) * gain

def ssd_scan(values, step_sizes, decay_rate, b_proj, c_proj, block_len):
    length, head_count, head_size = values.shape
    state_size = b_proj.shape[1]
    block_count = length // block_len
    rates = jnp.transpose((step_sizes * decay_rate).reshape(block_count, block_len, head_count), (0, 2, 1))
    weighted = (values * step_sizes[:, :, None]).reshape(block_count, block_len, head_count, head_size)
    b_blocks = b_proj.reshape(block_count, block_len, state_size)
    c_blocks = c_proj.reshape(block_count, block_len, state_size)
    cumulative = jnp.cumsum(rates, axis=2)
    gap_sums = cumulative[:, :, :, None] - cumulative[:, :, None, :]
    positions = jnp.arange(block_len)
    lower_mask = (positions[:, None] >= positions[None, :])[None, None, :, :]
    decay_kernel = jnp.where(lower_mask, jnp.exp(jnp.where(lower_mask, gap_sums, 0.0)), 0.0)
    scores = jnp.einsum('btn,bsn->bts', c_blocks, b_blocks, precision=highest)
    diag_out = jnp.einsum('bts,bhts,bshp->bthp', scores, decay_kernel, weighted, precision=highest)
    tail_decay = jnp.exp(cumulative[:, :, -1:] - cumulative)
    states = jnp.einsum('bhs,bshp,bsn->bhpn', tail_decay, weighted, b_blocks, precision=highest)
    block_decay = jnp.exp(cumulative[:, :, -1])

    def advance(running, item):
        fresh, factor = item
        return (running * factor[:, None, None] + fresh, running)
    start_state = jnp.zeros((head_count, head_size, state_size), jnp.float32)
    final_state, entering = lax.scan(advance, start_state, (states, block_decay))
    off_out = jnp.einsum('btn,bhpn,bht->bthp', c_blocks, entering, jnp.exp(cumulative), precision=highest)
    return (diag_out + off_out).reshape(length, head_count, head_size)

def mixer(projected, conv_weight, conv_bias, steps_bias, decay_log, skip_gain, diag_weight, second_gain):
    inner_width = second_gain.shape[0]
    width = conv_bias.shape[0]
    head_count = decay_log.shape[0]
    taps = conv_weight.shape[0]
    state_size = (width - inner_width) // 2
    length = projected.shape[0]
    gate_part = projected[:, :inner_width]
    conv_in = projected[:, inner_width:inner_width + width]
    raw_steps = projected[:, inner_width + width:]
    padded = jnp.pad(conv_in, ((taps - 1, 0), (0, 0)))
    conv_out = conv_bias + conv_weight[0] * padded[0:length]
    for offset in range(1, taps):
        conv_out = conv_out + conv_weight[offset] * padded[offset:offset + length]
    active = jax.nn.silu(conv_out)
    flat_values = active[:, :inner_width]
    values = flat_values.reshape(length, head_count, inner_width // head_count)
    b_proj = active[:, inner_width:inner_width + state_size]
    c_proj = active[:, inner_width + state_size:]
    steps_fwd = jax.nn.softplus(raw_steps[:, :head_count] + steps_bias[:head_count])
    steps_rev = jax.nn.softplus(raw_steps[:, head_count:] + steps_bias[head_count:])
    decay_rate = -jnp.exp(decay_log)
    forward_out = ssd_scan(values, steps_fwd, decay_rate, b_proj, c_proj, GROUP)
    reverse_out = jnp.flip(ssd_scan(jnp.flip(values, 0), jnp.flip(steps_rev, 0), decay_rate, jnp.flip(b_proj, 0), jnp.flip(c_proj, 0), GROUP), 0)
    shifted = jnp.pad(forward_out[:-1], ((1, 0), (0, 0), (0, 0))) + jnp.pad(reverse_out[1:], ((0, 1), (0, 0), (0, 0)))
    diagonal = skip_gain[None, :] + jnp.dot(flat_values, diag_weight, precision=highest)
    combined = shifted + diagonal[:, :, None] * values
    gated = combined.reshape(length, inner_width) * jax.nn.silu(gate_part)
    return rms_scale(gated, second_gain)

def layer_apply(current, params):
    first_gain, in_weight, conv_weight, conv_bias, second_gain, out_weight, steps_bias, decay_log, skip_gain, diag_weight = params
    normed = rms_scale(current, first_gain)
    projected = low_back(jnp.dot(low(normed), in_weight, precision=highest))
    hidden = low(mixer(projected, conv_weight, conv_bias, steps_bias, decay_log, skip_gain, diag_weight, second_gain))
    return current + low_back(jnp.dot(hidden, out_weight, precision=highest))

def reference(inputs, cotangent, norm_gain, in_w, conv_w, conv_b, dt_bias, a_log, skip, fc_d, inner_gain, out_w):
    params = tuple((member.astype(jnp.float32) for member in (norm_gain, in_w, conv_w, conv_b, inner_gain, out_w, dt_bias, a_log, skip, fc_d)))

    def model(tokens, weights):

        def one_sequence(unused_state, sequence):
            current = sequence
            for number in range(LAYERS):
                current = layer_apply(current, tuple((member[number] for member in weights)))
            return (unused_state, current)
        blocks = tokens.reshape(N_FSDP, SEQ, D)
        final_state, results = lax.scan(jax.checkpoint(one_sequence), jnp.zeros((), jnp.float32), blocks)
        return results.reshape(TOKENS, D)
    output, pullback = jax.vjp(model, inputs.astype(jnp.float32), params)
    grad_inputs, gradients = pullback(cotangent.astype(jnp.float32))
    return (output, grad_inputs, gradients[0], gradients[1], gradients[2], gradients[3], gradients[6], gradients[7], gradients[8], gradients[9], gradients[4], gradients[5])
```

```python
import functools

import jax
import jax.numpy as jnp
from jax import lax
from jax.experimental import pallas as pl
from jax.experimental.pallas import tpu as pltpu
from jax.sharding import PartitionSpec as P

Q = 128
EPS = 1e-05
F32 = jnp.float32
BF16 = jnp.bfloat16
NN = (((1,), (0,)), ((), ()))
NT = (((1,), (1,)), ((), ()))
TN = (((0,), (0,)), ((), ()))
MIB = 1024 * 1024


def mm(a, b, dims=NN):
    return lax.dot_general(
        a.astype(BF16), b.astype(BF16), dims, preferred_element_type=F32
    )


def split2(a):
    high = a.astype(BF16)
    return high, (a - high.astype(F32)).astype(BF16)


def mm_left(a, b, dims=NN):
    high, low = split2(a)
    return mm(high, b, dims) + mm(low, b, dims)


def mm3(a, b, dims=NN):
    ah, al = split2(a)
    bh, bl = split2(b)
    return mm(ah, bh, dims) + (mm(ah, bl, dims) + mm(al, bh, dims))


def exact(a, b, dims=NN):
    return lax.dot_general(
        a, b, dims, preferred_element_type=F32, precision=lax.Precision.HIGHEST
    )


def iota(shape, axis):
    return lax.broadcasted_iota(jnp.int32, shape, axis)


def sigmoid(v):
    return 1.0 / (1.0 + jnp.exp(-v))


def rows_of(b, size=Q):
    return pl.ds(pl.multiple_of(b * Q, Q), size)


def lanes_of(j, size=Q):
    return pl.ds(pl.multiple_of(j * size, size), size)


def spread_matrix(ref, heads, width):
    shape = ref.shape
    ref[...] = (iota(shape, 1) // width == iota(shape, 0) % heads).astype(F32).astype(BF16)


def spread(values, matrix):
    high = values.astype(BF16)
    rest = values - high.astype(F32)
    middle = rest.astype(BF16)
    low = (rest - middle.astype(F32)).astype(BF16)
    stacked = jnp.concatenate(
        [high.astype(F32), middle.astype(F32), low.astype(F32)], axis=0
    ).T.astype(BF16)
    return mm(stacked, matrix)


def head_sums(matrix, values):
    high, low = split2(values)
    return mm(matrix, high, NT) + mm(matrix, low, NT)


def step_terms(raw_t, bias, rate, heads):
    shifted = raw_t + bias
    steps = jnp.maximum(shifted, 0.0) + jnp.log1p(jnp.exp(-jnp.abs(shifted)))
    decay = steps * rate
    r, c = iota((Q, 2 * Q), 0), iota((Q, 2 * Q), 1)
    upto = jnp.where(c < Q, (r <= c).astype(F32), (r < c - Q).astype(F32))
    sums = exact(decay, upto)
    inc, exc = sums[:, :Q], sums[:, Q:]
    log_steps = jnp.maximum(jnp.log(steps), -200.0)
    return dict(
        shifted=shifted,
        steps=steps,
        f=inc[:heads],
        fe=exc[:heads],
        ri=inc[heads:],
        re=exc[heads:],
        row_f=inc[:heads] - log_steps[:heads],
        row_r=exc[heads:] + log_steps[heads:],
        f_last=jnp.sum(decay[:heads], axis=1, keepdims=True),
        r_last=jnp.sum(decay[heads:], axis=1, keepdims=True),
    )


def weights_of(terms, heads):
    ef = jnp.exp(terms["fe"])
    er = jnp.exp(jnp.minimum(terms["r_last"] - terms["ri"], 0.0))
    wf = jnp.exp(jnp.minimum(terms["f_last"] - terms["f"], 0.0)) * terms["steps"][:heads]
    wr = jnp.exp(terms["re"]) * terms["steps"][heads:]
    return ef, er, wf, wr


def conv_tile(ci_ref, cw_ref, cb_ref, b, j):
    window = ci_ref[rows_of(b, Q + 8), lanes_of(j)]
    taps = cw_ref.shape[0]
    total = cb_ref[:, lanes_of(j)].astype(F32)
    for k in range(taps):
        start = 8 - (taps - 1) + k
        total = total + cw_ref[k : k + 1, lanes_of(j)].astype(F32) * window[start : start + Q]
    return total


def activate(ci_ref, cw_ref, cb_ref, xs_ref, bc_ref, blocks, inner):
    tiles = inner // Q

    def block(b, carry):
        def tile(j, carry):
            v = conv_tile(ci_ref, cw_ref, cb_ref, b, j)
            xs_ref[rows_of(b), lanes_of(j)] = v / (1.0 + jnp.exp(-v))
            return carry

        lax.fori_loop(0, tiles, tile, 0)
        v = conv_tile(ci_ref, cw_ref, cb_ref, b, tiles)
        bc_ref[pl.ds(pl.multiple_of(b * Q + 8, 8), Q), :] = v / (1.0 + jnp.exp(-v))
        return carry

    zero8 = jnp.zeros((8, Q), F32)
    bc_ref[0:8, :] = zero8
    bc_ref[blocks * Q + 8 : blocks * Q + 16, :] = zero8
    lax.fori_loop(0, blocks, block, 0)


def shifted_bc(bc_ref, b):
    window = bc_ref[rows_of(b, Q + 16), :]
    state = Q // 2
    here = window[8 : 8 + Q]
    return here[:, :state], window[7 : 7 + Q][:, state:], window[9 : 9 + Q][:, state:]


def pair_diagonal(tile):
    lane = iota(tile.shape, 1)
    zero = jnp.zeros_like(tile)
    return jnp.concatenate(
        [jnp.where(lane < Q // 2, tile, zero), jnp.where(lane >= Q // 2, tile, zero)], axis=0
    )


def forward_mix_kernel(
    x_ref, g_ref, wb_ref, cw_ref, cb_ref, dtb_ref, alog_ref, skip_ref, fcd_ref,
    u_ref, ci_ref, rawt_ref, m_ref, s_ref, z_ref,
    xs_ref, bc_ref, wide_ref, narrow_ref, colf_ref, colr_ref, rowf_ref, rowr_ref,
):
    tokens, inner = m_ref.shape
    heads = alog_ref.shape[0]
    channels = cb_ref.shape[1]
    blocks = tokens // Q
    state = Q // 2
    ci_ref[0:8, :] = jnp.zeros((8, channels), F32)

    def project(b, carry):
        x = x_ref[rows_of(b), :].astype(F32)
        scale = lax.rsqrt(jnp.mean(x * x, axis=-1, keepdims=True) + EPS)
        u = (x * scale * g_ref[...].astype(F32)).astype(BF16)
        u_ref[rows_of(b), :] = u
        here = mm(u, wb_ref[...])
        ci_ref[pl.ds(pl.multiple_of(b * Q + 8, 8), Q), :] = here[:, :channels]
        raw = jnp.concatenate(
            [here[:, channels:], jnp.zeros((Q, Q - 2 * heads), F32)], axis=1
        )
        rawt_ref[:, rows_of(b)] = raw.T[: 2 * heads]
        return carry

    lax.fori_loop(0, blocks, project, 0)
    activate(ci_ref, cw_ref, cb_ref, xs_ref, bc_ref, blocks, inner)
    spread_matrix(wide_ref, heads, Q)
    spread_matrix(narrow_ref, heads, inner // heads)
    rate_one = -jnp.exp(alog_ref[...])
    rate = jnp.concatenate([rate_one, rate_one], axis=0)
    s_ref[0] = jnp.zeros((state, inner), F32)
    z_ref[blocks - 1] = jnp.zeros((state, inner), F32)

    def states(b, carry):
        terms = step_terms(rawt_ref[:, rows_of(b)], dtb_ref[...], rate, heads)
        ef, er, wf, wr = weights_of(terms, heads)
        x = xs_ref[rows_of(b), :]
        bmat, _, _ = shifted_bc(bc_ref, b)
        bt = bmat.T

        @pl.when(b < blocks - 1)
        def _():
            fresh = mm_left(bt, spread(wf, narrow_ref[...]) * x)
            factor = jnp.broadcast_to(jnp.exp(terms["f_last"]), (heads, Q))
            s_ref[b + 1] = s_ref[b] * spread(factor, narrow_ref[...])[0:1] + fresh

        @pl.when(b > 0)
        def _():
            z_ref[b - 1] = mm_left(bt, spread(wr, narrow_ref[...]) * x)

        return carry

    lax.fori_loop(0, blocks, states, 0)

    def later(i, carry):
        b = blocks - 2 - i
        terms = step_terms(rawt_ref[:, rows_of(b + 1)], dtb_ref[...], rate, heads)
        factor = jnp.broadcast_to(jnp.exp(terms["r_last"]), (heads, Q))
        z_ref[b] = z_ref[b] + z_ref[b + 1] * spread(factor, narrow_ref[...])[0:1]
        return carry

    lax.fori_loop(0, blocks - 1, later, 0)

    def mix(b, carry):
        terms = step_terms(rawt_ref[:, rows_of(b)], dtb_ref[...], rate, heads)
        ef, er, wf, wr = weights_of(terms, heads)
        colf_ref[...] = spread(terms["fe"], wide_ref[...])
        colr_ref[...] = spread(terms["ri"], wide_ref[...])
        rowf_ref[...] = terms["row_f"]
        rowr_ref[...] = terms["row_r"]
        x = xs_ref[rows_of(b), :]
        bmat, cdn, cup = shifted_bc(bc_ref, b)
        diag = head_sums(fcd_ref[...].astype(F32), x) + skip_ref[...]
        off = spread(diag, narrow_ref[...]) * x
        off = off + spread(ef, narrow_ref[...]) * mm_left(cdn, s_ref[b])
        off = off + spread(er, narrow_ref[...]) * mm_left(cup, z_ref[b])
        m_ref[rows_of(b), :] = off
        t, s = iota((Q, Q), 0), iota((Q, Q), 1)
        lower = s < t
        gram = jnp.where(lower, exact(cdn, bmat, NT), exact(cup, bmat, NT))
        gram = jnp.where(s == t, 0.0, gram)

        def pair(p, carry):
            kernels = []
            for j in range(2):
                h = 2 * p + j
                gaps = jnp.where(
                    lower,
                    colf_ref[:, lanes_of(h)] - rowf_ref[pl.ds(h, 1), :],
                    rowr_ref[pl.ds(h, 1), :] - colr_ref[:, lanes_of(h)],
                )
                kernels.append((gram * jnp.exp(jnp.minimum(gaps, 60.0))).astype(BF16))
            tile = xs_ref[rows_of(b), lanes_of(p)].astype(BF16)
            m_ref[rows_of(b), lanes_of(p)] += mm(
                jnp.concatenate(kernels, axis=1), pair_diagonal(tile)
            )
            return carry

        lax.fori_loop(0, heads // 2, pair, 0)
        return carry

    lax.fori_loop(0, blocks, mix, 0)


def forward_mix(x, gain, wb, cw, cb, dtb, alog, skip, fcd_t):
    tokens, width = x.shape
    channels = cb.shape[1]
    heads = alog.shape[0]
    state = Q // 2
    inner = channels - 2 * state
    blocks = tokens // Q
    return pl.pallas_call(
        forward_mix_kernel,
        name="forward_mix",
        out_shape=(
            jax.ShapeDtypeStruct((tokens, width), BF16),
            jax.ShapeDtypeStruct((tokens + 8, channels), F32),
            jax.ShapeDtypeStruct((2 * heads, tokens), F32),
            jax.ShapeDtypeStruct((tokens, inner), F32),
            jax.ShapeDtypeStruct((blocks, state, inner), F32),
            jax.ShapeDtypeStruct((blocks, state, inner), F32),
        ),
        scratch_shapes=[
            pltpu.VMEM((tokens, inner), F32),
            pltpu.VMEM((tokens + 16, Q), F32),
            pltpu.VMEM((3 * heads, heads * Q), BF16),
            pltpu.VMEM((3 * heads, inner), BF16),
            pltpu.VMEM((Q, heads * Q), F32),
            pltpu.VMEM((Q, heads * Q), F32),
            pltpu.VMEM((heads, Q), F32),
            pltpu.VMEM((heads, Q), F32),
        ],
        compiler_params=pltpu.CompilerParams(vmem_limit_bytes=56 * MIB),
        cost_estimate=pl.CostEstimate(
            flops=60_000_000_000, bytes_accessed=20_000_000, transcendentals=4_000_000
        ),
    )(x, gain, wb, cw, cb, dtb, alog, skip, fcd_t)


def forward_out_kernel(x_ref, u_ref, m_ref, wa_ref, g_ref, wo_ref, z_ref, hid_ref, y_ref):
    blocks = m_ref.shape[0] // Q

    def block(b, carry):
        z = mm(u_ref[rows_of(b), :], wa_ref[...])
        z_ref[rows_of(b), :] = z
        v = m_ref[rows_of(b), :] * (z / (1.0 + jnp.exp(-z)))
        scale = lax.rsqrt(jnp.mean(v * v, axis=-1, keepdims=True) + EPS)
        hid = (v * scale * g_ref[...].astype(F32)).astype(BF16)
        hid_ref[rows_of(b), :] = hid
        y_ref[rows_of(b), :] = x_ref[rows_of(b), :].astype(F32) + mm(hid, wo_ref[...])
        return carry

    lax.fori_loop(0, blocks, block, 0)


def forward_out(x, u, m, wa, gain, wo):
    tokens, width = x.shape
    inner = m.shape[1]
    return pl.pallas_call(
        forward_out_kernel,
        name="forward_out",
        out_shape=(
            jax.ShapeDtypeStruct((tokens, inner), F32),
            jax.ShapeDtypeStruct((tokens, inner), BF16),
            jax.ShapeDtypeStruct((tokens, width), F32),
        ),
        compiler_params=pltpu.CompilerParams(vmem_limit_bytes=56 * MIB),
        cost_estimate=pl.CostEstimate(
            flops=12_000_000_000, bytes_accessed=20_000_000, transcendentals=800_000
        ),
    )(x, u, m, wa, gain, wo)


def backward_out_kernel(
    g_ref, wo_ref, z_ref, m_ref, gain_ref, wa_ref, gb_ref, dm_ref, dz_ref, dn_ref, dgain_ref
):
    tokens, inner = m_ref.shape
    blocks = tokens // Q
    dgain_ref[...] = jnp.zeros((1, inner), F32)

    def block(b, carry):
        gb = g_ref[rows_of(b), :].astype(BF16)
        gb_ref[rows_of(b), :] = gb
        dhid = mm(gb, wo_ref[...], NT)
        z = z_ref[rows_of(b), :]
        m = m_ref[rows_of(b), :]
        s = sigmoid(z)
        v = m * (z * s)
        scale = lax.rsqrt(jnp.mean(v * v, axis=-1, keepdims=True) + EPS)
        dgain_ref[...] += jnp.sum(dhid * (v * scale), axis=0, keepdims=True)
        dvn = dhid * gain_ref[...].astype(F32)
        pull = jnp.mean(dvn * v, axis=-1, keepdims=True) * (scale * scale * scale)
        dv = dvn * scale - v * pull
        dm_ref[rows_of(b), :] = dv * (z * s)
        dz = (dv * m * (s * (1.0 + z * (1.0 - s)))).astype(BF16)
        dz_ref[rows_of(b), :] = dz
        dn_ref[rows_of(b), :] = mm(dz, wa_ref[...], NT)
        return carry

    lax.fori_loop(0, blocks, block, 0)


def backward_out(g, wo, z, m, gain, wa):
    tokens, width = g.shape
    inner = m.shape[1]
    return pl.pallas_call(
        backward_out_kernel,
        name="backward_out",
        out_shape=(
            jax.ShapeDtypeStruct((tokens, width), BF16),
            jax.ShapeDtypeStruct((tokens, inner), F32),
            jax.ShapeDtypeStruct((tokens, inner), BF16),
            jax.ShapeDtypeStruct((tokens, width), F32),
            jax.ShapeDtypeStruct((1, inner), F32),
        ),
        compiler_params=pltpu.CompilerParams(vmem_limit_bytes=56 * MIB),
        cost_estimate=pl.CostEstimate(
            flops=12_000_000_000, bytes_accessed=20_000_000, transcendentals=800_000
        ),
    )(g, wo, z, m, gain, wa)


def backward_mix_kernel(
    ci_ref, rawt_ref, dm_ref, s_ref, z_ref, cw_ref, cb_ref, dtb_ref, alog_ref, skip_ref, fcd_ref,
    dp_ref, dcw_ref, dcb_ref, ddtb_ref, dalog_ref, dskip_ref, dfcd_ref,
    xs_ref, bc_ref, wide_ref, narrow_ref, cola_ref, colb_ref, rowa_ref, rowb_ref,
    ds_ref, dz_ref, dx_ref, db_ref, dcd_ref, dcu_ref, dgram_ref, sums_ref, dconv_ref,
):
    tokens, inner = dm_ref.shape
    heads = alog_ref.shape[0]
    channels = cb_ref.shape[1]
    taps = cw_ref.shape[0]
    blocks = tokens // Q
    state = Q // 2
    activate(ci_ref, cw_ref, cb_ref, xs_ref, bc_ref, blocks, inner)
    spread_matrix(wide_ref, heads, Q)
    spread_matrix(narrow_ref, heads, inner // heads)
    rate_one = -jnp.exp(alog_ref[...])
    rate = jnp.concatenate([rate_one, rate_one], axis=0)
    one_hot = narrow_ref[0:heads, :]
    dalog_ref[...] = jnp.zeros_like(dalog_ref)
    ddtb_ref[...] = jnp.zeros_like(ddtb_ref)
    dskip_ref[...] = jnp.zeros_like(dskip_ref)
    dfcd_ref[...] = jnp.zeros_like(dfcd_ref)
    zero8 = jnp.zeros((8, state), F32)
    for ref in (dcd_ref, dcu_ref):
        ref[0:8, :] = zero8
        ref[tokens + 8 : tokens + 16, :] = zero8

    def wide_sum(values):
        return head_sums(one_hot, values)

    def state_grads(b, carry):
        terms = step_terms(rawt_ref[:, rows_of(b)], dtb_ref[...], rate, heads)
        ef, er, wf, wr = weights_of(terms, heads)
        dm = dm_ref[rows_of(b), :]
        _, cdn, cup = shifted_bc(bc_ref, b)
        ds_ref[b] = mm_left(cdn.T, spread(ef, narrow_ref[...]) * dm)
        own = mm_left(cup.T, spread(er, narrow_ref[...]) * dm)

        @pl.when(b == 0)
        def _():
            dz_ref[0] = own

        @pl.when(b > 0)
        def _():
            factor = jnp.broadcast_to(jnp.exp(terms["r_last"]), (heads, Q))
            dz_ref[b] = own + dz_ref[b - 1] * spread(factor, narrow_ref[...])[0:1]

        return carry

    lax.fori_loop(0, blocks, state_grads, 0)

    def earlier(i, carry):
        b = blocks - 2 - i
        terms = step_terms(rawt_ref[:, rows_of(b)], dtb_ref[...], rate, heads)
        factor = jnp.broadcast_to(jnp.exp(terms["f_last"]), (heads, Q))
        ds_ref[b] = ds_ref[b] + ds_ref[b + 1] * spread(factor, narrow_ref[...])[0:1]
        return carry

    lax.fori_loop(0, blocks - 1, earlier, 0)

    def block(b, carry):
        terms = step_terms(rawt_ref[:, rows_of(b)], dtb_ref[...], rate, heads)
        ef, er, wf, wr = weights_of(terms, heads)
        cola_ref[...] = spread(terms["row_f"], wide_ref[...])
        colb_ref[...] = spread(terms["row_r"], wide_ref[...])
        rowa_ref[...] = terms["fe"]
        rowb_ref[...] = terms["ri"]
        x = xs_ref[rows_of(b), :]
        dm = dm_ref[rows_of(b), :]
        bmat, cdn, cup = shifted_bc(bc_ref, b)

        diag = head_sums(fcd_ref[...].astype(F32), x) + skip_ref[...]
        ddiag = wide_sum(dm * x)
        dskip_ref[...] += jnp.sum(ddiag, axis=1, keepdims=True)
        dfcd_ref[...] += mm(ddiag, x)
        dx = spread(diag, narrow_ref[...]) * dm
        tall = jnp.concatenate([ddiag, jnp.zeros((Q - heads, Q), F32)], axis=0).T
        dx = dx + mm_left(tall[:, :heads], fcd_ref[...])

        zf = spread(ef, narrow_ref[...]) * dm
        rho_f = wide_sum(zf * mm_left(cdn, s_ref[b]))
        dcdn = mm(zf, s_ref[b], NT)
        zr = spread(er, narrow_ref[...]) * dm
        rho_r = wide_sum(zr * mm_left(cup, z_ref[b]))
        dcup = mm(zr, z_ref[b], NT)

        later_on = (b < blocks - 1).astype(F32)
        dsn = ds_ref[jnp.minimum(b + 1, blocks - 1)] * later_on
        wfx = spread(wf, narrow_ref[...])
        vf = mm_left(bmat, dsn)
        omega_f = wide_sum(wfx * x * vf)
        dx = dx + wfx * vf
        db = mm(wfx * x, dsn, NT)
        last_f = jnp.exp(terms["f_last"]) * jnp.sum(wide_sum(dsn * s_ref[b]), axis=1, keepdims=True)

        earlier_on = (b > 0).astype(F32)
        dzn = dz_ref[jnp.maximum(b - 1, 0)] * earlier_on
        wrx = spread(wr, narrow_ref[...])
        vr = mm_left(bmat, dzn)
        omega_r = wide_sum(wrx * x * vr)
        dx = dx + wrx * vr
        db = db + mm(wrx * x, dzn, NT)
        last_r = jnp.exp(terms["r_last"]) * jnp.sum(wide_sum(dzn * z_ref[b]), axis=1, keepdims=True)
        dx_ref[...] = dx

        s, t = iota((Q, Q), 0), iota((Q, Q), 1)
        lower = s < t
        gram = jnp.where(lower, exact(bmat, cdn, NT), exact(bmat, cup, NT))
        gram = jnp.where(s == t, 0.0, gram)
        r2, c2 = iota((Q, 2 * Q), 0), iota((Q, 2 * Q), 1)
        beside = jnp.where(c2 < Q, (r2 > c2).astype(F32), (r2 < c2 - Q).astype(F32)).astype(BF16)
        dgram_ref[...] = jnp.zeros((Q, Q), F32)

        def pair(p, carry):
            tile = xs_ref[rows_of(b), lanes_of(p)].astype(BF16)
            dpair = pair_diagonal(dm_ref[rows_of(b), lanes_of(p)].astype(BF16))
            outer = mm(tile, dpair, NT)
            kernels, weights = [], []
            grown = dgram_ref[...]
            for j in range(2):
                h = 2 * p + j
                gaps = jnp.where(
                    lower,
                    rowa_ref[pl.ds(h, 1), :] - cola_ref[:, lanes_of(h)],
                    colb_ref[:, lanes_of(h)] - rowb_ref[pl.ds(h, 1), :],
                )
                decay = jnp.exp(jnp.minimum(gaps, 60.0))
                kernels.append((gram * decay).astype(BF16))
                product = decay * outer[:, j * Q : (j + 1) * Q]
                grown = grown + product
                weights.append((gram * product).astype(BF16))
            dgram_ref[...] = grown
            dx_ref[:, lanes_of(p)] += mm(jnp.concatenate(kernels, axis=1), dpair)
            for j in range(2):
                h = 2 * p + j
                spans = mm(weights[j], beside)
                after, before = spans[:, :Q], spans[:, Q:]
                sums_ref[0, pl.ds(h, 1), :] = jnp.sum(jnp.where(s < t, after, 0.0), axis=0, keepdims=True)
                sums_ref[1, pl.ds(h, 1), :] = jnp.sum(jnp.where(s > t, before, 0.0), axis=0, keepdims=True)
                sums_ref[2, pl.ds(h, 1), :] = jnp.sum(jnp.where(s == t, after, 0.0), axis=0, keepdims=True)
                sums_ref[3, pl.ds(h, 1), :] = jnp.sum(jnp.where(s == t, before, 0.0), axis=0, keepdims=True)
            return carry

        lax.fori_loop(0, heads // 2, pair, 0)
        xs_ref[rows_of(b), :] = dx_ref[...]

        grown = dgram_ref[...]
        low = jnp.where(lower, grown, 0.0)
        high = jnp.where(s > t, grown, 0.0)
        db = db + mm_left(low, cdn) + mm_left(high, cup)
        db_ref[rows_of(b), :] = db
        dcd_ref[pl.ds(pl.multiple_of(b * Q + 8, 8), Q), :] = dcdn + mm_left(low.T, bmat)
        dcu_ref[pl.ds(pl.multiple_of(b * Q + 8, 8), Q), :] = dcup + mm_left(high.T, bmat)

        r, c = iota((Q, Q), 0), iota((Q, Q), 1)
        above = (r > c).astype(F32)
        below = (r < c).astype(F32)
        da_f = sums_ref[0] + exact(rho_f, above) + exact(omega_f, below) + last_f
        da_r = sums_ref[1] + exact(rho_r, below) + exact(omega_r, above) + last_r
        steps = terms["steps"]
        slope = sigmoid(terms["shifted"])
        ratio = jnp.where(steps > 0.0, slope / jnp.where(steps > 0.0, steps, 1.0), 1.0)
        direct = jnp.concatenate([sums_ref[2] + omega_f, sums_ref[3] + omega_r], axis=0)
        da = jnp.concatenate([da_f, da_r], axis=0)
        draw = direct * ratio + da * rate * slope
        ddtb_ref[...] += jnp.sum(draw, axis=1, keepdims=True)
        both = da * steps
        dalog_ref[...] += rate_one * jnp.sum(both[:heads] + both[heads:], axis=1, keepdims=True)
        padded = jnp.concatenate([draw, jnp.zeros((Q - 2 * heads, Q), F32)], axis=0)
        dp_ref[rows_of(b), channels:] = padded.T[:, : 2 * heads].astype(BF16)
        return carry

    lax.fori_loop(0, blocks, block, 0)

    dconv_ref[tokens : tokens + 8, :] = jnp.zeros((8, channels), F32)
    dcw_ref[...] = jnp.zeros_like(dcw_ref)
    dcb_ref[...] = jnp.zeros_like(dcb_ref)
    tiles = inner // Q

    def pull_tile(b, j, dact):
        v = conv_tile(ci_ref, cw_ref, cb_ref, b, j)
        s = sigmoid(v)
        dconv = dact * (s * (1.0 + v * (1.0 - s)))
        dconv_ref[rows_of(b), lanes_of(j)] = dconv
        dcb_ref[:, lanes_of(j)] += jnp.sum(dconv, axis=0, keepdims=True)
        window = ci_ref[rows_of(b, Q + 8), lanes_of(j)]
        for k in range(taps):
            start = 8 - (taps - 1) + k
            dcw_ref[k : k + 1, lanes_of(j)] += jnp.sum(
                dconv * window[start : start + Q], axis=0, keepdims=True
            )

    def pull_block(b, carry):
        def tile(j, carry):
            pull_tile(b, j, xs_ref[rows_of(b), lanes_of(j)])
            return carry

        lax.fori_loop(0, tiles, tile, 0)
        down = dcd_ref[rows_of(b, Q + 16), :]
        up = dcu_ref[rows_of(b, Q + 16), :]
        dc = down[9 : 9 + Q] + up[7 : 7 + Q]
        pull_tile(b, tiles, jnp.concatenate([db_ref[rows_of(b), :], dc], axis=1))
        return carry

    lax.fori_loop(0, blocks, pull_block, 0)

    def spread_block(b, carry):
        def tile(j, carry):
            window = dconv_ref[rows_of(b, Q + 8), lanes_of(j)]
            total = jnp.zeros((Q, Q), F32)
            for k in range(taps):
                start = taps - 1 - k
                total = total + cw_ref[k : k + 1, lanes_of(j)].astype(F32) * window[start : start + Q]
            dp_ref[rows_of(b), lanes_of(j)] = total.astype(BF16)
            return carry

        lax.fori_loop(0, channels // Q, tile, 0)
        return carry

    lax.fori_loop(0, blocks, spread_block, 0)


def backward_mix(ci, rawt, dm, s, z, cw, cb, dtb, alog, skip, fcd_t):
    tokens, inner = dm.shape
    channels = cb.shape[1]
    heads = alog.shape[0]
    state = Q // 2
    blocks = tokens // Q
    return pl.pallas_call(
        backward_mix_kernel,
        name="backward_mix",
        out_shape=(
            jax.ShapeDtypeStruct((tokens, channels + 2 * heads), BF16),
            jax.ShapeDtypeStruct(cw.shape, F32),
            jax.ShapeDtypeStruct((1, channels), F32),
            jax.ShapeDtypeStruct((2 * heads, 1), F32),
            jax.ShapeDtypeStruct((heads, 1), F32),
            jax.ShapeDtypeStruct((heads, 1), F32),
            jax.ShapeDtypeStruct((heads, inner), F32),
        ),
        scratch_shapes=[
            pltpu.VMEM((tokens, inner), F32),
            pltpu.VMEM((tokens + 16, Q), F32),
            pltpu.VMEM((3 * heads, heads * Q), BF16),
            pltpu.VMEM((3 * heads, inner), BF16),
            pltpu.VMEM((Q, heads * Q), F32),
            pltpu.VMEM((Q, heads * Q), F32),
            pltpu.VMEM((heads, Q), F32),
            pltpu.VMEM((heads, Q), F32),
            pltpu.VMEM((blocks, state, inner), F32),
            pltpu.VMEM((blocks, state, inner), F32),
            pltpu.VMEM((Q, inner), F32),
            pltpu.VMEM((tokens, state), F32),
            pltpu.VMEM((tokens + 16, state), F32),
            pltpu.VMEM((tokens + 16, state), F32),
            pltpu.VMEM((Q, Q), F32),
            pltpu.VMEM((4, heads, Q), F32),
            pltpu.VMEM((tokens + 8, channels), F32),
        ],
        compiler_params=pltpu.CompilerParams(vmem_limit_bytes=56 * MIB),
        cost_estimate=pl.CostEstimate(
            flops=100_000_000_000, bytes_accessed=30_000_000, transcendentals=8_000_000
        ),
    )(ci, rawt, dm, s, z, cw, cb, dtb, alog, skip, fcd_t)


def backward_norm_kernel(g_ref, x_ref, gain_ref, dn_ref, dp_ref, wb_ref, dx_ref, dgain_ref):
    tokens, width = x_ref.shape
    blocks = tokens // Q
    dgain_ref[...] = jnp.zeros((1, width), F32)

    def block(b, carry):
        dn = dn_ref[rows_of(b), :] + mm(dp_ref[rows_of(b), :], wb_ref[...], NT)
        x = x_ref[rows_of(b), :].astype(F32)
        scale = lax.rsqrt(jnp.mean(x * x, axis=-1, keepdims=True) + EPS)
        dgain_ref[...] += jnp.sum(dn * (x * scale), axis=0, keepdims=True)
        dvn = dn * gain_ref[...].astype(F32)
        pull = jnp.mean(dvn * x, axis=-1, keepdims=True) * (scale * scale * scale)
        dx_ref[rows_of(b), :] = g_ref[rows_of(b), :].astype(F32) + dvn * scale - x * pull
        return carry

    lax.fori_loop(0, blocks, block, 0)


def backward_norm(g, x, gain, dn, dp, wb):
    tokens, width = x.shape
    return pl.pallas_call(
        backward_norm_kernel,
        name="backward_norm",
        out_shape=(
            jax.ShapeDtypeStruct((tokens, width), F32),
            jax.ShapeDtypeStruct((1, width), F32),
        ),
        compiler_params=pltpu.CompilerParams(vmem_limit_bytes=56 * MIB),
        cost_estimate=pl.CostEstimate(
            flops=3_000_000_000, bytes_accessed=9_000_000, transcendentals=0
        ),
    )(g, x, gain, dn, dp, wb)


def bit_count(n):
    return n.bit_length() - 1


def gather_blocks(block, axis_name, order):
    n = lax.axis_size(axis_name)
    bits = bit_count(n)
    if n != 1 << bits:
        return lax.all_gather(block, axis_name, axis=0, tiled=False)
    me = lax.axis_index(axis_name)
    cur = block.reshape((1,) * bits + block.shape)
    for b in order(bits):
        pairs = [(i, i ^ (1 << b)) for i in range(n)]
        other = lax.ppermute(cur, axis_name, pairs)
        axis = bits - 1 - b
        cur = jnp.where(
            (me >> b) % 2 == 0,
            jnp.concatenate([cur, other], axis=axis),
            jnp.concatenate([other, cur], axis=axis),
        )
    return cur.reshape((n,) + block.shape)


def scatter_blocks(blocks, axis_name, order, wire):
    n = lax.axis_size(axis_name)
    bits = bit_count(n)
    if n != 1 << bits:
        return lax.psum_scatter(blocks, axis_name, scatter_dimension=0, tiled=False)
    me = lax.axis_index(axis_name)
    shape = blocks.shape[1:]
    cur = blocks.reshape((2,) * bits + shape)
    for b in order(bits):
        pairs = [(i, i ^ (1 << b)) for i in range(n)]
        axis = bits - 1 - b
        mine = (me >> b) % 2
        keep = lax.dynamic_slice_in_dim(cur, mine, 1, axis)
        send = lax.dynamic_slice_in_dim(cur, 1 - mine, 1, axis).astype(wire)
        cur = keep + lax.ppermute(send, axis_name, pairs).astype(F32)
    return cur.reshape(shape)


def gather_order(bits):
    return list(range(bits - 1, -1, -1))


def scatter_order(bits):
    return list(range(bits))


def wgrad(a, b):
    return lax.dot_general(a, b, TN, preferred_element_type=F32)


def shards(
    inputs, cotangent, norm_gain, in_w, conv_w, conv_b, dt_bias, a_log, skip, fc_d, inner_gain, out_w
):
    n = lax.axis_size("fsdp")
    layers = in_w.shape[0]
    inner = inner_gain.shape[1] * n
    channels = conv_b.shape[1] * n
    width = inputs.shape[1]
    heads = a_log.shape[1]
    taps = conv_w.shape[1]
    proj = in_w.shape[2]

    small = jnp.concatenate(
        [
            member.reshape(layers, -1)
            for member in (norm_gain, conv_w, conv_b, inner_gain, fc_d)
        ],
        axis=1,
    )
    sizes = [norm_gain[0].size, conv_w[0].size, conv_b[0].size, inner_gain[0].size, fc_d[0].size]
    cuts = [sum(sizes[:i]) for i in range(len(sizes) + 1)]
    small = gather_blocks(small, "fsdp", gather_order)

    full = []
    for l in range(layers):
        wb = gather_blocks(in_w[l, :, inner:], "fsdp", gather_order).reshape(width, proj - inner)
        wa = gather_blocks(in_w[l, :, :inner], "fsdp", gather_order).reshape(width, inner)
        wo = gather_blocks(out_w[l], "fsdp", gather_order).reshape(inner, width)
        parts = [small[:, l, cuts[i] : cuts[i + 1]] for i in range(len(sizes))]
        g1 = parts[0].reshape(1, width)
        cw = parts[1].reshape(n, taps, -1).transpose(1, 0, 2).reshape(taps, channels)
        cb = parts[2].reshape(1, channels)
        g2 = parts[3].reshape(1, inner)
        fcd_t = parts[4].reshape(inner, heads).T
        full.append((g1, cw, cb, g2, fcd_t, wb, wa, wo))

    current = inputs
    saved = []
    for l in range(layers):
        g1, cw, cb, g2, fcd_t, wb, wa, wo = full[l]
        heads_in = (dt_bias[l][:, None], a_log[l][:, None], skip[l][:, None])
        u, ci, rawt, m, s, z = forward_mix(current, g1, wb, cw, cb, *heads_in, fcd_t)
        gate, hid, following = forward_out(current, u, m, wa, g2, wo)
        saved.append((current, u, ci, rawt, m, s, z, gate, hid, heads_in))
        current = following
    output = current

    upstream = cotangent
    big = [None] * layers
    little = [None] * layers
    for l in reversed(range(layers)):
        g1, cw, cb, g2, fcd_t, wb, wa, wo = full[l]
        x, u, ci, rawt, m, s, z, gate, hid, heads_in = saved[l]
        gb, dm, dz, dn, dg2 = backward_out(upstream, wo, gate, m, g2, wa)
        dwo = scatter_blocks(wgrad(hid, gb).reshape(n, -1, width), "fsdp", scatter_order, BF16)
        dwa = scatter_blocks(wgrad(u, dz).reshape(n, -1, inner), "fsdp", scatter_order, BF16)
        dp, dcw, dcb, ddtb, dalog, dskip, dfcd = backward_mix(
            ci, rawt, dm, s, z, cw, cb, *heads_in, fcd_t
        )
        dwb = scatter_blocks(
            wgrad(u, dp).reshape(n, -1, proj - inner), "fsdp", scatter_order, BF16
        )
        upstream, dg1 = backward_norm(upstream, x, g1, dn, dp, wb)
        big[l] = (jnp.concatenate([dwa, dwb], axis=1), dwo)
        little[l] = jnp.concatenate(
            [
                dg1.reshape(n, -1),
                dcw.reshape(taps, n, -1).transpose(1, 0, 2).reshape(n, -1),
                dcb.reshape(n, -1),
                dg2.reshape(n, -1),
                dfcd.T.reshape(n, -1),
                jnp.broadcast_to(
                    jnp.concatenate([ddtb[:, 0], dalog[:, 0], dskip[:, 0]])[None], (n, 4 * heads)
                ),
            ],
            axis=1,
        )
    total = scatter_blocks(jnp.stack(little, axis=1), "fsdp", scatter_order, F32)
    sizes = sizes + [2 * heads, heads, heads]
    cuts = [sum(sizes[:i]) for i in range(len(sizes) + 1)]
    parts = [total[:, cuts[i] : cuts[i + 1]] for i in range(len(sizes))]
    return (
        output,
        upstream,
        parts[0],
        jnp.stack([big[l][0] for l in range(layers)]),
        parts[1].reshape(conv_w.shape),
        parts[2],
        parts[5],
        parts[6],
        parts[7],
        parts[4].reshape(fc_d.shape),
        parts[3],
        jnp.stack([big[l][1] for l in range(layers)]),
    )


def solution(mesh):
    rows = P("fsdp", None)
    second = P(None, "fsdp")
    return jax.shard_map(
        shards,
        mesh=mesh,
        in_specs=(
            rows, rows, second, P(None, "fsdp", None), P(None, None, "fsdp"), second,
            P(), P(), P(), P(None, "fsdp", None), second, P(None, "fsdp", None),
        ),
        out_specs=(
            rows, rows, second, P(None, "fsdp", None), P(None, None, "fsdp"), second,
            P(), P(), P(), P(None, "fsdp", None), second, P(None, "fsdp", None),
        ),
        check_vma=False,
    )
```
